32 devices in a mesh: groups: 2 (over y), area: 8 (over z, x), row: 2 (over core).
Axes of the slice: x: 2, y: 2, z: 4, core: 2. Of those that a mesh axis runs over, the one named last changes fastest.
Arguments:
- proj_index: int32 [8, 384], P('area', 'row'), may hold values from 0 to 2047
- delays: int32 [8, 2], P('area'), may hold values from 3 to 5
- past_rates: bfloat16 [8, 6, 128, 384], P('area', None, 'groups', 'row'), parts along dimension 2, may hold values from -0.8984375 to 0.8984375
- potential: float32 [8, 128, 4096], P('area', 'groups', 'row'), parts along dimension 1, may hold values from -6 to 6
- stimulus: float32 [8, 128, 4096], P('area', 'groups', 'row'), parts along dimension 1, may hold values from -5 to 5
- leak_rate: float32 [8, 4096], P('area', 'row'), may hold values from 0.1 to 0.6
- recurrence: bfloat16 [8, 4096, 4096], P('area', None, 'row'), may hold values from -0.09375 to 0.09375
- ff_weight: bfloat16 [8, 192, 4096], P('area', None, 'row'), may hold values from -0.4375 to 0.4375
- fb_weight: bfloat16 [8, 192, 4096], P('area', None, 'row'), may hold values from -0.4375 to 0.4375
Outputs:
- final_potential: float32 [8, 128, 4096], P('area', 'groups', 'row'), parts along dimension 1
The draws below stay inside these ranges and needn't reach their ends.
There are 2 independent parts, one for each index of `groups`. The reference program is written for one: setup_inputs(seed, part) draws one part's arguments, and reference() takes and returns one part's arrays. A program takes and returns all parts, laid end to end along the dimension named above; an argument that names none is the same for every part. Nothing has to cross between parts.
Inputs may be any that keep to these rules, and one draw needn't show every extreme that they name: `proj_index`: indices within a block of 2048 neurons.
All inputs are finite; a program needn't handle non-finite values.
Results may differ from the reference program's by a relative error of at most 0.0013.
Values may be sent and summed in bfloat16 or wider, within the bound.
A program may use at most 64 MiB of HBM per device.

```python
import math
import jax
import jax.numpy as jnp
from jax import lax

NEU = 4096
PROJ = 192
TR = 64
SUB = 3
OUTER = 2
AREAS = 8
PROJS = 384
N_ROW = 2


def with_ends(values, stream_key, smallest, largest):
    extent = values.shape
    spot = [jax.random.randint(jax.random.fold_in(stream_key, axis), (), 0, extent[axis]) for axis in range(len(extent))]
    values = values.at[tuple(spot)].set(smallest)
    longest = extent.index(max(extent))
    spot[longest] = (spot[longest] + 1) % extent[longest]
    return values.at[tuple(spot)].set(largest)


def levels(stream_key, extent, shards, least, high):
    factor_of, own = 1.0, jax.random.fold_in(stream_key, 6)
    for dim, shards_of in shards:
        draws = jnp.exp(jax.random.uniform(jax.random.fold_in(own, dim), (shards_of,), jnp.float32, least / len(shards), high / len(shards)))
        factor_of = factor_of * jnp.repeat(draws, extent[dim] // shards_of).reshape([-1 if axis == dim else 1 for axis in range(len(extent))])
    return factor_of


def centred(stream_key, extent, deviation, reach, shards=(), kind=jnp.bfloat16):
    factor_of = levels(stream_key, extent, shards, -0.22, 0.18) if shards else 1.0
    array = jax.random.normal(stream_key, extent, jnp.float32) * deviation * factor_of
    return jnp.minimum(jnp.maximum(array, -reach), reach).astype(kind)


def setup_inputs(seed: int = 0, part: int = 0) -> dict:
    streams_of = jax.random.split(jax.random.key(seed), 10)
    part_splits = jax.random.split(jax.random.fold_in(streams_of[9], part), 10)
    proj_index = with_ends(jax.random.randint(streams_of[0], (AREAS, PROJS), 0, NEU // N_ROW), jax.random.fold_in(streams_of[0], 1), 0, (NEU // N_ROW) - 1).astype(jnp.int32)
    delays = with_ends(jax.random.randint(streams_of[1], (AREAS, 2), SUB, 2 * SUB), jax.random.fold_in(streams_of[1], 1), SUB, (2 * SUB) - 1).astype(jnp.int32)
    past_rates = jnp.clip(jax.random.uniform(part_splits[2], (AREAS, 2 * SUB, TR, PROJS), jnp.float32, -0.8984375, 0.8984375) * levels(part_splits[2], (AREAS, 2 * SUB, TR, PROJS), ((0, 8), (3, 2)), -0.4, 0.0), -0.8984375, 0.8984375).astype(jnp.bfloat16)
    potential = centred(part_splits[3], (AREAS, TR, NEU), 1.0, 6.0, ((0, 8), (2, 2)), jnp.float32)
    stimulus = centred(part_splits[4], (AREAS, TR, NEU), 0.7, 5.0, ((0, 8), (2, 2)), jnp.float32)
    leak_rate = jnp.clip(jnp.exp(math.log(0.6) - 1.7917595 * jax.random.uniform(streams_of[5], (AREAS, NEU), jnp.float32) ** levels(streams_of[5], (AREAS, NEU), ((0, 8), (1, 2)), -0.2, 0.2)), 0.1, 0.6)
    recurrence = centred(streams_of[6], (AREAS, NEU, NEU), NEU ** -0.5, 0.09375, ((0, 8), (2, 2)))
    ff_weight = centred(streams_of[7], (AREAS, PROJ, NEU), PROJ ** -0.5, 0.4375, ((0, 8), (2, 2)))
    fb_weight = centred(streams_of[8], (AREAS, PROJ, NEU), PROJ ** -0.5, 0.4375, ((0, 8), (2, 2)))
    return dict(proj_index=proj_index, delays=delays, past_rates=past_rates, potential=potential, stimulus=stimulus, leak_rate=leak_rate, recurrence=recurrence, ff_weight=ff_weight, fb_weight=fb_weight)


def incoming(stacked, direction, lag_steps, mapping, instant):
    source = jnp.roll(stacked, direction, axis=0)
    position = (instant + 2 * SUB - lag_steps).astype(jnp.int32)
    selected_index = jnp.take_along_axis(source, position[:, None, None, None], axis=1)[:, 0]
    area_count = selected_index.shape[0]
    trials = selected_index.shape[1]
    grouped = selected_index.reshape(area_count, trials, N_ROW, PROJ).astype(jnp.float32)
    mapping_blocks = mapping.reshape(area_count, PROJ, N_ROW, NEU // N_ROW).astype(jnp.float32)
    return jnp.einsum("atrj,ajrn->atrn", grouped, mapping_blocks).reshape(area_count, trials, NEU)


def reference(proj_index, delays, past_rates, potential, stimulus, leak_rate, recurrence, ff_weight, fb_weight):
    block_rows = NEU // N_ROW
    offsets = (jnp.arange(PROJ * N_ROW, dtype=jnp.int32) // PROJ) * block_rows
    global_index = (proj_index + offsets[None, :]).astype(jnp.int32)
    area_count = potential.shape[0]
    trials = potential.shape[1]
    delay_table = jnp.broadcast_to(global_index[:, None, :], (area_count, trials, PROJ * N_ROW))
    history = [past_rates[:, position] for position in range(2 * SUB)]
    membrane_voltage = potential
    for instant in range(OUTER * SUB):
        spiking_rates = jnp.tanh(membrane_voltage).astype(jnp.bfloat16)
        selected_rows = jnp.take_along_axis(spiking_rates, delay_table, axis=2)
        stacked = jnp.stack(history, axis=1)
        forward = incoming(stacked, 1, delays[:, 0], ff_weight, instant)
        backward = incoming(stacked, -1, delays[:, 1], fb_weight, instant)
        history.append(selected_rows)
        recurrent_drive = lax.map(lambda product_factors: jnp.dot(product_factors[0], product_factors[1], preferred_element_type=jnp.float32), (spiking_rates, recurrence))
        membrane_voltage = membrane_voltage + leak_rate[:, None, :] * (-membrane_voltage + recurrent_drive + forward + backward + stimulus)
    return membrane_voltage
```

```python
import functools

import jax
import jax.numpy as jnp
from jax import lax
from jax.experimental import pallas as pl
from jax.experimental.pallas import tpu as pltpu
from jax.sharding import PartitionSpec as P

SUB = 3
OUTER = 2
STEPS = SUB * OUTER
WIDTH = 1024
LANES = 128
PAIR = 2
GROUP = 4
MESH = pl.DeviceIdType.MESH
F32 = jnp.float32
BF16 = jnp.bfloat16


def dot(a, b):
    return jnp.dot(a, b, preferred_element_type=F32)


def kernel(
    areas,
    delays, index, past, potential, stimulus, leak, recurrence, ff, fb,
    out,
    w_own, w_far, maps, x, stim, leak_v, index_v, acc, own, far, onehot, past_v, sent, proj, hist_a, hist_b,
    in_sems, w_sems, send_sems, recv_sems, ring_send, ring_a, ring_b,
):
    half, lanes = w_own.shape[1:]
    chunks, width = own.shape[1], own.shape[3]
    blocks = half // lanes
    per = width // lanes
    groups = blocks // GROUP
    trials = x.shape[0]
    half_trials = trials // 2
    projecting = index_v.shape[1]
    rest = projecting - lanes
    row = lax.axis_index("row")
    area = lax.axis_index("area")
    partner = {"row": 1 - row}
    ahead = {"area": lax.rem(area + 1, areas)}
    behind = {"area": lax.rem(area + areas - 1, areas)}

    barrier = pltpu.get_barrier_semaphore()
    for peer in (ahead, behind, partner):
        pl.semaphore_signal(barrier, inc=1, device_id=peer, device_id_type=MESH)

    def local_copy(source, target, sem):
        copy = pltpu.make_async_copy(source, target, sem)
        copy.start()
        return copy

    get_past = local_copy(past.at[0], past_v, in_sems.at[0])
    get_x = local_copy(potential.at[0], x, in_sems.at[1])
    get_index = local_copy(index, index_v, in_sems.at[2])
    own_row = pl.multiple_of(row * half, half)
    far_row = pl.multiple_of((1 - row) * half, half)

    def load_group(target, first_row, g, sem):
        for b in range(g * GROUP, (g + 1) * GROUP):
            pltpu.make_async_copy(
                recurrence.at[0, pl.ds(first_row, half), pl.ds(b * lanes, lanes)], target.at[b], w_sems.at[sem]
            ).start()

    def wait_group(target, g, sem):
        slots = target.at[pl.ds(g * GROUP, GROUP)]
        pltpu.make_async_copy(slots, slots, w_sems.at[sem]).wait()

    for g in range(groups):
        load_group(w_own, own_row, g, g)
    get_stim = local_copy(stimulus.at[0], stim, in_sems.at[3])
    get_leak = local_copy(leak, leak_v, in_sems.at[4])

    def load_maps():
        for d, weights in enumerate((ff, fb)):
            pltpu.make_async_copy(weights.at[0], maps.at[d, pl.ds(0, projecting)], in_sems.at[5]).start()
            pltpu.make_async_copy(
                weights.at[0, pl.ds(lanes, rest)], maps.at[d, pl.ds(projecting, rest)], in_sems.at[5]
            ).start()

    def wait_maps():
        pltpu.make_async_copy(maps, maps, in_sems.at[5]).wait()

    def send_rates(i, c):
        return pltpu.make_async_remote_copy(
            src_ref=own.at[i, c], dst_ref=far.at[i, c],
            send_sem=send_sems.at[i, c], recv_sem=recv_sems.at[i, c],
            device_id=partner, device_id_type=MESH,
        )

    def send_ring(source, first, count, group):
        slots = pl.ds(first, count)
        return (
            pltpu.make_async_remote_copy(
                src_ref=source, dst_ref=hist_a.at[slots],
                send_sem=ring_send.at[0, group], recv_sem=ring_a.at[group],
                device_id=ahead, device_id_type=MESH,
            ),
            pltpu.make_async_remote_copy(
                src_ref=source, dst_ref=hist_b.at[slots],
                send_sem=ring_send.at[1, group], recv_sem=ring_b.at[group],
                device_id=behind, device_id_type=MESH,
            ),
        )

    def ring_group(g):
        if g == 0:
            return send_ring(sent.at[pl.ds(0, SUB)], 0, SUB, 0)
        if g < SUB:
            return send_ring(sent.at[pl.ds(SUB + g - 1, 1)], SUB + g - 1, 1, g)
        return send_ring(proj.at[pl.ds(g - SUB, 1)], SUB + g - 1, 1, g)

    low = lax.broadcasted_iota(jnp.int32, (half_trials, lanes), 1) < rest

    def gather(i):
        total = dot(own[i, 0], onehot[0])
        for c in range(1, chunks):
            total += dot(own[i, c], onehot[c])
        tail = total[:, lanes:]
        proj[i, 0:trials] = total[:, :lanes].astype(BF16)
        proj[i, trials:] = jnp.where(low, tail[:half_trials], tail[half_trials:]).astype(BF16)

    def select(hist, i, d):
        packed = jnp.where(d == SUB, hist[i + 2], jnp.where(d == SUB + 1, hist[i + 1], hist[i]))
        tail = packed[trials:].astype(F32)
        tail = jnp.concatenate([jnp.where(low, tail, 0.0), jnp.where(low, 0.0, tail)], axis=0).astype(BF16)
        return jnp.concatenate([packed[:trials], tail], axis=1)

    def product(rates, i, weights, c):
        parts = []
        for b in range(c * per, (c + 1) * per, PAIR):
            total = None
            for k in range(chunks):
                rows = slice(k * width, (k + 1) * width)
                tile = jnp.concatenate([weights[b + p, rows] for p in range(PAIR)], axis=1)
                term = dot(rates[i, k], tile)
                total = term if total is None else total + term
            parts.append(total)
        return jnp.concatenate(parts, axis=1)

    get_past.wait()
    for s in range(1, STEPS):
        values = past_v[s].astype(F32)
        tail = values[:, lanes:]
        sent[s - 1, 0:trials] = values[:, :lanes].astype(BF16)
        sent[s - 1, trials:] = jnp.concatenate([tail[:half_trials], tail[half_trials:]], axis=1).astype(BF16)
    pl.semaphore_wait(barrier, 3)
    for copy in ring_group(0):
        copy.start()
    get_x.wait()
    for c in range(chunks):
        own[0, c] = jnp.tanh(x[:, c * width:(c + 1) * width]).astype(BF16)
        send_rates(0, c).start()
    for g in range(1, SUB):
        for copy in ring_group(g):
            copy.start()
    get_index.wait()
    spread = index_v[0:1, :]
    spread = jnp.concatenate([spread, spread[:, lanes:]], axis=1)
    for c in range(chunks):
        spots = lax.broadcasted_iota(jnp.int32, (width, spread.shape[1]), 0) + c * width
        onehot[c] = jnp.where(spots == spread, 1.0, 0.0).astype(BF16)
    gather(0)
    for copy in ring_group(SUB):
        copy.start()

    for i in range(STEPS):
        first = i == 0
        if 0 < i < SUB:
            gather(i)
            for copy in ring_group(SUB + i):
                copy.start()
        if first:
            get_stim.wait()
            get_leak.wait()
        for c in range(chunks):
            cols = slice(c * width, (c + 1) * width)
            if first:
                for g in range(c * per // GROUP, (c + 1) * per // GROUP):
                    wait_group(w_own, g, g)
                    load_group(w_far, far_row, g, groups + g)
                if c == 0:
                    load_maps()
            acc[:, cols] = stim[:, cols] + product(own, i, w_own, c)

        def couple():
            for copy in ring_group(i):
                copy.wait_recv()
            return jnp.concatenate([select(hist_a, i, delays[0, 0]), select(hist_b, i, delays[0, 1])], axis=1)

        def coupled(rates, c):
            cols = slice(c * width, (c + 1) * width)
            depth = maps.shape[1]
            return dot(rates[:, :depth], maps[0, :, cols]) + dot(rates[:, depth:], maps[1, :, cols])

        if first:
            for c in range(chunks):
                send_rates(0, c).wait_recv()
            for c in range(chunks):
                cols = slice(c * width, (c + 1) * width)
                for g in range(c * per // GROUP, (c + 1) * per // GROUP):
                    wait_group(w_far, g, groups + g)
                acc[:, cols] += product(far, i, w_far, c)
            wait_maps()
            arrived = couple()
        else:
            arrived = couple()
            for c in range(chunks):
                cols = slice(c * width, (c + 1) * width)
                acc[:, cols] += coupled(arrived, c)
            for c in range(chunks):
                send_rates(i, c).wait_recv()
        for c in range(chunks):
            cols = slice(c * width, (c + 1) * width)
            if first:
                drive = acc[:, cols] + coupled(arrived, c)
            else:
                drive = acc[:, cols] + product(far, i, w_far, c)
            now = x[:, cols]
            new = now + leak_v[:, cols] * (drive - now)
            if i + 1 < STEPS:
                x[:, cols] = new
                own[i + 1, c] = jnp.tanh(new).astype(BF16)
                send_rates(i + 1, c).start()
            else:
                out[0, :, cols] = new
    for i in range(STEPS):
        for c in range(chunks):
            send_rates(i, c).wait_send()
        for copy in ring_group(i):
            copy.wait_send()


def local(areas, proj_index, delays, past_rates, potential, stimulus, leak_rate, recurrence, ff_weight, fb_weight):
    _, trials, block = potential.shape
    projecting = proj_index.shape[1]
    width = min(WIDTH, block)
    chunks = block // width
    depth = 2 * projecting - LANES
    packed = trials + trials // 2
    anywhere = pl.BlockSpec(memory_space=pl.ANY)
    vmem = pltpu.VMEM
    dma = pltpu.SemaphoreType.DMA
    return pl.pallas_call(
        functools.partial(kernel, areas),
        out_shape=vmem(potential.shape, F32),
        in_specs=[pl.BlockSpec(memory_space=pltpu.SMEM)] + [anywhere] * 8,
        out_specs=pl.BlockSpec(memory_space=vmem),
        scratch_shapes=[
            vmem((block // LANES, block, LANES), BF16),
            vmem((block // LANES, block, LANES), BF16),
            vmem((2, depth, block), BF16),
            vmem((trials, block), F32),
            vmem((trials, block), F32),
            vmem((1, block), F32),
            vmem((1, projecting), jnp.int32),
            vmem((trials, block), F32),
            vmem((STEPS, chunks, trials, width), BF16),
            vmem((STEPS, chunks, trials, width), BF16),
            vmem((chunks, width, depth), BF16),
            vmem(past_rates.shape[1:], BF16),
            vmem((STEPS - 1, packed, LANES), BF16),
            vmem((SUB, packed, LANES), BF16),
            vmem((STEPS + 2, packed, LANES), BF16),
            vmem((STEPS + 2, packed, LANES), BF16),
            dma((6,)),
            dma((2 * (block // LANES) // GROUP,)),
            dma((STEPS, chunks)),
            dma((STEPS, chunks)),
            dma((2, STEPS)),
            dma((STEPS,)),
            dma((STEPS,)),
        ],
        compiler_params=pltpu.CompilerParams(
            collective_id=0, has_side_effects=True, vmem_limit_bytes=66_000_000
        ),
        name="loop_dynamics",
    )(delays, *(
        pltpu.with_memory_space_constraint(array, pltpu.HBM)
        for array in (proj_index, past_rates, potential, stimulus, leak_rate, recurrence, ff_weight, fb_weight)
    ))


def solution(mesh):
    return jax.shard_map(
        functools.partial(local, mesh.shape["area"]),
        mesh=mesh,
        in_specs=(
            P("area", "row"),
            P("area", None),
            P("area", None, "groups", "row"),
            P("area", "groups", "row"),
            P("area", "groups", "row"),
            P("area", "row"),
            P("area", None, "row"),
            P("area", None, "row"),
            P("area", None, "row"),
        ),
        out_specs=P("area", "groups", "row"),
        check_vma=False,
    )
```

```python
import functools

import jax
import jax.numpy as jnp
from jax import lax
from jax.experimental import pallas as pl
from jax.experimental.pallas import tpu as pltpu
from jax.sharding import PartitionSpec as P

SUB = 3
OUTER = 2
STEPS = SUB * OUTER
WIDTH = 1024
LANES = 128
PAIR = 2
ROWS = 128
MESH = pl.DeviceIdType.MESH
F32 = jnp.float32
BF16 = jnp.bfloat16


def dot(a, b):
    rows, depth = a.shape
    if rows < ROWS:
        a = jnp.concatenate([a, jnp.zeros((ROWS - rows, depth), a.dtype)], axis=0)
    return jnp.dot(a, b, preferred_element_type=F32)[:rows]


def kernel(
    areas,
    delays, index, past, potential, stimulus, leak, recurrence, ff, fb,
    out,
    w_own, w_far, maps, x, stim, leak_v, index_v, acc, own, far, onehot, past_v, sent, proj, hist_a, hist_b,
    in_sems, w_sems, sent_sem, recv_sems, ring_send, ring_recv,
):
    half, lanes = w_own.shape[1:]
    chunks, width = own.shape[1], own.shape[3]
    blocks = half // lanes
    per = width // lanes
    trials = x.shape[0]
    half_trials = trials // 2
    projecting = index_v.shape[1]
    rest = projecting - lanes
    row = lax.axis_index("row")
    area = lax.axis_index("area")
    partner = {"row": 1 - row}
    ahead = {"area": lax.rem(area + 1, areas)}
    behind = {"area": lax.rem(area + areas - 1, areas)}

    barrier = pltpu.get_barrier_semaphore()
    for peer in (ahead, behind, partner):
        pl.semaphore_signal(barrier, inc=1, device_id=peer, device_id_type=MESH)

    def local_copy(source, target, sem):
        copy = pltpu.make_async_copy(source, target, sem)
        copy.start()
        return copy

    get_past = local_copy(past.at[0], past_v, in_sems.at[0])
    get_x = local_copy(potential.at[0], x, in_sems.at[1])
    get_index = local_copy(index, index_v, in_sems.at[2])
    own_row = pl.multiple_of(row * half, half)
    far_row = pl.multiple_of((1 - row) * half, half)

    def load(target, first_row, c, sem):
        for b in range(c * per, (c + 1) * per):
            pltpu.make_async_copy(
                recurrence.at[0, pl.ds(first_row, half), pl.ds(b * lanes, lanes)], target.at[b], w_sems.at[sem]
            ).start()

    def wait_bytes(ref, sem):
        pltpu.make_async_copy(ref, ref, sem).wait()

    def loaded(target, c, sem):
        wait_bytes(target.at[pl.ds(c * per, per)], w_sems.at[sem])

    def load_maps():
        for d, weights in enumerate((ff, fb)):
            pltpu.make_async_copy(weights.at[0], maps.at[d, pl.ds(0, projecting)], in_sems.at[5]).start()
            pltpu.make_async_copy(
                weights.at[0, pl.ds(lanes, rest)], maps.at[d, pl.ds(projecting, rest)], in_sems.at[5]
            ).start()

    def send_rates(i, c):
        return pltpu.make_async_remote_copy(
            src_ref=own.at[i, c], dst_ref=far.at[i, c],
            send_sem=sent_sem, recv_sem=recv_sems.at[i],
            device_id=partner, device_id_type=MESH,
        )

    def send_ring(source, first, count, group):
        slots = pl.ds(first, count)
        return (
            pltpu.make_async_remote_copy(
                src_ref=source, dst_ref=hist_a.at[slots],
                send_sem=ring_send.at[0], recv_sem=ring_recv.at[group],
                device_id=ahead, device_id_type=MESH,
            ),
            pltpu.make_async_remote_copy(
                src_ref=source, dst_ref=hist_b.at[slots],
                send_sem=ring_send.at[1], recv_sem=ring_recv.at[group],
                device_id=behind, device_id_type=MESH,
            ),
        )

    def ring_group(g):
        if g == 0:
            return send_ring(sent.at[pl.ds(0, SUB)], 0, SUB, 0)
        if g < SUB:
            return send_ring(sent.at[pl.ds(SUB + g - 1, 1)], SUB + g - 1, 1, g)
        return send_ring(proj.at[pl.ds(g - SUB, 1)], SUB + g - 1, 1, g)

    low = lax.broadcasted_iota(jnp.int32, (half_trials, lanes), 1) < rest

    def gather(i):
        total = dot(own[i, 0], onehot[0])
        for c in range(1, chunks):
            total += dot(own[i, c], onehot[c])
        tail = total[:, lanes:]
        proj[i, 0:trials] = total[:, :lanes].astype(BF16)
        proj[i, trials:] = jnp.where(low, tail[:half_trials], tail[half_trials:]).astype(BF16)

    def select(hist, i, d):
        packed = jnp.where(d == SUB, hist[i + 2], jnp.where(d == SUB + 1, hist[i + 1], hist[i]))
        tail = packed[trials:].astype(F32)
        tail = jnp.concatenate([jnp.where(low, tail, 0.0), jnp.where(low, 0.0, tail)], axis=0).astype(BF16)
        return jnp.concatenate([packed[:trials], tail], axis=1)

    def product(rates, i, weights, c, arrived=None):
        parts = []
        for b in range(c * per, (c + 1) * per, PAIR):
            total = None
            for k in range(chunks):
                rows = slice(k * width, (k + 1) * width)
                tile = jnp.concatenate([weights[b + p, rows] for p in range(PAIR)], axis=1)
                term = dot(rates[i, k], tile)
                total = term if total is None else total + term
            if arrived is not None:
                total += coupled(arrived, b)
            parts.append(total)
        return jnp.concatenate(parts, axis=1)

    get_past.wait()
    for s in range(1, STEPS):
        values = past_v[s].astype(F32)
        tail = values[:, lanes:]
        sent[s - 1, 0:trials] = values[:, :lanes].astype(BF16)
        sent[s - 1, trials:] = jnp.concatenate([tail[:half_trials], tail[half_trials:]], axis=1).astype(BF16)
    for c in range(chunks):
        load(w_own, own_row, c, c)
    pl.semaphore_wait(barrier, 3)
    for copy in ring_group(0):
        copy.start()
    get_x.wait()
    for c in range(chunks):
        own[0, c] = jnp.tanh(x[:, c * width:(c + 1) * width]).astype(BF16)
        send_rates(0, c).start()
    load(w_far, far_row, 0, chunks)
    get_stim = local_copy(stimulus.at[0], stim, in_sems.at[3])
    get_leak = local_copy(leak, leak_v, in_sems.at[4])
    for g in range(1, SUB):
        for copy in ring_group(g):
            copy.start()
    get_index.wait()
    spread = index_v[0:1, :]
    spread = jnp.concatenate([spread, spread[:, lanes:]], axis=1)
    for c in range(chunks):
        spots = lax.broadcasted_iota(jnp.int32, (width, spread.shape[1]), 0) + c * width
        onehot[c] = jnp.where(spots == spread, 1.0, 0.0).astype(BF16)
    gather(0)
    for copy in ring_group(SUB):
        copy.start()

    def couple(i):
        count = 2 * SUB if i == 0 else 2
        wait_bytes(hist_a.at[pl.ds(0, count)], ring_recv.at[i])
        return jnp.concatenate([select(hist_a, i, delays[0, 0]), select(hist_b, i, delays[0, 1])], axis=1)

    def coupled(rates, b):
        cols = slice(b * lanes, (b + PAIR) * lanes)
        return dot(rates, jnp.concatenate([maps[d, :, cols] for d in range(2)], axis=0))

    def update(i, c, drive):
        cols = slice(c * width, (c + 1) * width)
        now = x[:, cols]
        new = now + leak_v[:, cols] * (drive - now)
        if i + 1 < STEPS:
            x[:, cols] = new
            own[i + 1, c] = jnp.tanh(new).astype(BF16)
            send_rates(i + 1, c).start()
        else:
            out[0, :, cols] = new

    for c in range(chunks):
        loaded(w_own, c, c)
        if c + 1 < chunks:
            load(w_far, far_row, c + 1, chunks + c + 1)
        if c == 0:
            load_maps()
        acc[:, c * width:(c + 1) * width] = product(own, 0, w_own, c)
    wait_bytes(far.at[0], recv_sems.at[0])
    get_stim.wait()
    get_leak.wait()
    for c in range(chunks):
        cols = slice(c * width, (c + 1) * width)
        loaded(w_far, c, chunks + c)
        acc[:, cols] += stim[:, cols] + product(far, 0, w_far, c)
    wait_bytes(maps, in_sems.at[5])
    arrived = couple(0)
    for c in range(chunks):
        terms = [coupled(arrived, b) for b in range(c * per, (c + 1) * per, PAIR)]
        update(0, c, acc[:, c * width:(c + 1) * width] + jnp.concatenate(terms, axis=1))

    for i in range(1, STEPS):
        if i < SUB:
            gather(i)
            for copy in ring_group(SUB + i):
                copy.start()
        for c in range(chunks):
            cols = slice(c * width, (c + 1) * width)
            acc[:, cols] = stim[:, cols] + product(own, i, w_own, c)
        arrived = couple(i)
        wait_bytes(far.at[i], recv_sems.at[i])
        for c in range(chunks):
            cols = slice(c * width, (c + 1) * width)
            update(i, c, acc[:, cols] + product(far, i, w_far, c, arrived))
    wait_bytes(own, sent_sem)
    wait_bytes(hist_a, ring_send.at[0])
    wait_bytes(hist_b, ring_send.at[1])


def local(areas, proj_index, delays, past_rates, potential, stimulus, leak_rate, recurrence, ff_weight, fb_weight):
    _, trials, block = potential.shape
    projecting = proj_index.shape[1]
    width = min(WIDTH, block)
    chunks = block // width
    depth = 2 * projecting - LANES
    packed = trials + trials // 2
    anywhere = pl.BlockSpec(memory_space=pl.ANY)
    vmem = pltpu.VMEM
    dma = pltpu.SemaphoreType.DMA
    return pl.pallas_call(
        functools.partial(kernel, areas),
        out_shape=vmem(potential.shape, F32),
        in_specs=[pl.BlockSpec(memory_space=pltpu.SMEM)] + [anywhere] * 8,
        out_specs=pl.BlockSpec(memory_space=vmem),
        scratch_shapes=[
            vmem((block // LANES, block, LANES), BF16),
            vmem((block // LANES, block, LANES), BF16),
            vmem((2, depth, block), BF16),
            vmem((trials, block), F32),
            vmem((trials, block), F32),
            vmem((1, block), F32),
            vmem((1, projecting), jnp.int32),
            vmem((trials, block), F32),
            vmem((STEPS, chunks, trials, width), BF16),
            vmem((STEPS, chunks, trials, width), BF16),
            vmem((chunks, width, depth), BF16),
            vmem(past_rates.shape[1:], BF16),
            vmem((STEPS - 1, packed, LANES), BF16),
            vmem((SUB, packed, LANES), BF16),
            vmem((STEPS + 2, packed, LANES), BF16),
            vmem((STEPS + 2, packed, LANES), BF16),
            dma((6,)),
            dma((2 * chunks,)),
            dma,
            dma((STEPS,)),
            dma((2,)),
            dma((STEPS,)),
        ],
        compiler_params=pltpu.CompilerParams(
            collective_id=0, has_side_effects=True, vmem_limit_bytes=66_000_000
        ),
        name="loop_dynamics",
    )(delays, *(
        pltpu.with_memory_space_constraint(array, pltpu.HBM)
        for array in (proj_index, past_rates, potential, stimulus, leak_rate, recurrence, ff_weight, fb_weight)
    ))


def solution(mesh):
    return jax.shard_map(
        functools.partial(local, mesh.shape["area"]),
        mesh=mesh,
        in_specs=(
            P("area", "row"),
            P("area", None),
            P("area", None, "groups", "row"),
            P("area", "groups", "row"),
            P("area", "groups", "row"),
            P("area", "row"),
            P("area", None, "row"),
            P("area", None, "row"),
            P("area", None, "row"),
        ),
        out_specs=P("area", "groups", "row"),
        check_vma=False,
    )
```

```python
import functools

import jax
import jax.numpy as jnp
from jax import lax
from jax.experimental import pallas as pl
from jax.experimental.pallas import tpu as pltpu
from jax.sharding import PartitionSpec as P

SUB = 3
OUTER = 2
STEPS = SUB * OUTER
WIDTH = 1024
LANES = 128
PAIR = 2
ROWS = 128
MESH = pl.DeviceIdType.MESH
F32 = jnp.float32
BF16 = jnp.bfloat16


def dot(a, b):
    rows, depth = a.shape
    if rows < ROWS:
        a = jnp.concatenate([a, jnp.zeros((ROWS - rows, depth), a.dtype)], axis=0)
    return jnp.dot(a, b, preferred_element_type=F32)[:rows]


def kernel(
    areas,
    delays_in, index, past, potential, stimulus, leak, recurrence, ff, fb,
    out,
    w_own, w_far, maps, x, stim, leak_v, index_v, acc, own, far, onehot, delays, past_v, sent, proj, hist_a, hist_b,
    in_sems, w_sems, sent_sem, recv_sems, ring_send, ring_recv,
):
    half, lanes = w_own.shape[1:]
    chunks, width = own.shape[1], own.shape[3]
    blocks = half // lanes
    per = width // lanes
    trials = x.shape[0]
    half_trials = trials // 2
    projecting = index_v.shape[1]
    rest = projecting - lanes
    row = lax.axis_index("row")
    area = lax.axis_index("area")
    partner = {"row": 1 - row}
    ahead = {"area": lax.rem(area + 1, areas)}
    behind = {"area": lax.rem(area + areas - 1, areas)}

    barrier = pltpu.get_barrier_semaphore()
    for peer in (ahead, behind, partner):
        pl.semaphore_signal(barrier, inc=1, device_id=peer, device_id_type=MESH)

    def local_copy(source, target, sem):
        copy = pltpu.make_async_copy(source, target, sem)
        copy.start()
        return copy

    get_past = local_copy(past.at[0], past_v, in_sems.at[0])
    get_x = local_copy(potential.at[0], x, in_sems.at[1])
    get_index = local_copy(index, index_v, in_sems.at[2])
    get_delays = local_copy(delays_in, delays, in_sems.at[6])
    own_row = pl.multiple_of(row * half, half)
    far_row = pl.multiple_of((1 - row) * half, half)

    def load(target, first_row, c, sem):
        for b in range(c * per, (c + 1) * per):
            pltpu.make_async_copy(
                recurrence.at[0, pl.ds(first_row, half), pl.ds(b * lanes, lanes)], target.at[b], w_sems.at[sem]
            ).start()

    def wait_bytes(ref, sem):
        pltpu.make_async_copy(ref, ref, sem).wait()

    def loaded(target, c, sem):
        wait_bytes(target.at[pl.ds(c * per, per)], w_sems.at[sem])

    def load_maps():
        for d, weights in enumerate((ff, fb)):
            pltpu.make_async_copy(weights.at[0], maps.at[d, pl.ds(0, projecting)], in_sems.at[5]).start()
            pltpu.make_async_copy(
                weights.at[0, pl.ds(lanes, rest)], maps.at[d, pl.ds(projecting, rest)], in_sems.at[5]
            ).start()

    def send_rates(i, c):
        return pltpu.make_async_remote_copy(
            src_ref=own.at[i, c], dst_ref=far.at[i, c],
            send_sem=sent_sem, recv_sem=recv_sems.at[i],
            device_id=partner, device_id_type=MESH,
        )

    def send_ring(source, first, count, group):
        slots = pl.ds(first, count)
        return (
            pltpu.make_async_remote_copy(
                src_ref=source, dst_ref=hist_a.at[slots],
                send_sem=ring_send.at[0], recv_sem=ring_recv.at[group],
                device_id=ahead, device_id_type=MESH,
            ),
            pltpu.make_async_remote_copy(
                src_ref=source, dst_ref=hist_b.at[slots],
                send_sem=ring_send.at[1], recv_sem=ring_recv.at[group],
                device_id=behind, device_id_type=MESH,
            ),
        )

    def ring_group(g):
        if g == 0:
            return send_ring(sent.at[pl.ds(0, SUB)], 0, SUB, 0)
        if g < SUB:
            return send_ring(sent.at[pl.ds(SUB + g - 1, 1)], SUB + g - 1, 1, g)
        return send_ring(proj.at[pl.ds(g - SUB, 1)], SUB + g - 1, 1, g)

    low = lax.broadcasted_iota(jnp.int32, (half_trials, lanes), 1) < rest

    def gather(i):
        total = dot(own[i, 0], onehot[0])
        for c in range(1, chunks):
            total += dot(own[i, c], onehot[c])
        tail = total[:, lanes:]
        proj[i, 0:trials] = total[:, :lanes].astype(BF16)
        proj[i, trials:] = jnp.where(low, tail[:half_trials], tail[half_trials:]).astype(BF16)

    def select(hist, i, d):
        packed = jnp.where(d == SUB, hist[i + 2], jnp.where(d == SUB + 1, hist[i + 1], hist[i]))
        tail = packed[trials:].astype(F32)
        tail = jnp.concatenate([jnp.where(low, tail, 0.0), jnp.where(low, 0.0, tail)], axis=0).astype(BF16)
        return jnp.concatenate([packed[:trials], tail], axis=1)

    def product(rates, i, weights, b):
        total = None
        for k in range(chunks):
            rows = slice(k * width, (k + 1) * width)
            tile = jnp.concatenate([weights[b + p, rows] for p in range(PAIR)], axis=1)
            term = dot(rates[i, k], tile)
            total = term if total is None else total + term
        return total

    def pairs(c):
        for b in range(c * per, (c + 1) * per, PAIR):
            yield b, slice(b * lanes, (b + PAIR) * lanes)

    get_past.wait()
    for s in range(1, STEPS):
        values = past_v[s].astype(F32)
        tail = values[:, lanes:]
        sent[s - 1, 0:trials] = values[:, :lanes].astype(BF16)
        sent[s - 1, trials:] = jnp.concatenate([tail[:half_trials], tail[half_trials:]], axis=1).astype(BF16)
    for c in range(chunks):
        load(w_own, own_row, c, c)
    get_stim = local_copy(stimulus.at[0], stim, in_sems.at[3])
    get_leak = local_copy(leak, leak_v, in_sems.at[4])
    load(w_far, far_row, 0, chunks)
    pl.semaphore_wait(barrier, 3)
    for copy in ring_group(0):
        copy.start()
    get_x.wait()
    for c in range(chunks):
        own[0, c] = jnp.tanh(x[:, c * width:(c + 1) * width]).astype(BF16)
        send_rates(0, c).start()
    for c in range(1, chunks):
        load(w_far, far_row, c, chunks + c)
    load_maps()
    for g in range(1, SUB):
        for copy in ring_group(g):
            copy.start()
    def couple(i):
        count = 2 * SUB if i == 0 else 2
        wait_bytes(hist_a.at[pl.ds(0, count)], ring_recv.at[i])
        return jnp.concatenate([select(hist_a, i, delays[0, 0]), select(hist_b, i, delays[0, 1])], axis=1)

    def coupled(rates, cols):
        return dot(rates, jnp.concatenate([maps[d, :, cols] for d in range(2)], axis=0))

    def update(i, c, cols, drive):
        now = x[:, cols]
        new = now + leak_v[:, cols] * (drive - now)
        if i + 1 < STEPS:
            x[:, cols] = new
            own[i + 1, c, :, cols.start - c * width:cols.stop - c * width] = jnp.tanh(new).astype(BF16)
        else:
            out[0, :, cols] = new

    for c in range(chunks):
        loaded(w_own, c, c)
        for b, cols in pairs(c):
            acc[:, cols] = product(own, 0, w_own, b)
    get_index.wait()
    spread = index_v[0:1, :]
    spread = jnp.concatenate([spread, spread[:, lanes:]], axis=1)
    for c in range(chunks):
        spots = lax.broadcasted_iota(jnp.int32, (width, spread.shape[1]), 0) + c * width
        onehot[c] = jnp.where(spots == spread, 1.0, 0.0).astype(BF16)
    gather(0)
    for copy in ring_group(SUB):
        copy.start()
    wait_bytes(far.at[0], recv_sems.at[0])
    get_stim.wait()
    get_leak.wait()
    for c in range(chunks):
        loaded(w_far, c, chunks + c)
        for b, cols in pairs(c):
            acc[:, cols] += stim[:, cols] + product(far, 0, w_far, b)
    wait_bytes(maps, in_sems.at[5])
    get_delays.wait()
    arrived = couple(0)
    for c in range(chunks):
        for b, cols in pairs(c):
            update(0, c, cols, acc[:, cols] + coupled(arrived, cols))
        send_rates(1, c).start()

    for i in range(1, STEPS):
        if i < SUB:
            gather(i)
            for copy in ring_group(SUB + i):
                copy.start()
        for c in range(chunks):
            for b, cols in pairs(c):
                acc[:, cols] = stim[:, cols] + product(own, i, w_own, b)
        arrived = couple(i)
        wait_bytes(far.at[i], recv_sems.at[i])
        for c in range(chunks):
            for b, cols in pairs(c):
                update(i, c, cols, acc[:, cols] + product(far, i, w_far, b) + coupled(arrived, cols))
            if i + 1 < STEPS:
                send_rates(i + 1, c).start()
    wait_bytes(own, sent_sem)
    wait_bytes(hist_a, ring_send.at[0])
    wait_bytes(hist_b, ring_send.at[1])


def local(areas, proj_index, delays, past_rates, potential, stimulus, leak_rate, recurrence, ff_weight, fb_weight):
    _, trials, block = potential.shape
    projecting = proj_index.shape[1]
    width = min(WIDTH, block)
    chunks = block // width
    depth = 2 * projecting - LANES
    packed = trials + trials // 2
    anywhere = pl.BlockSpec(memory_space=pl.ANY)
    vmem = pltpu.VMEM
    dma = pltpu.SemaphoreType.DMA
    return pl.pallas_call(
        functools.partial(kernel, areas),
        out_shape=vmem(potential.shape, F32),
        in_specs=[anywhere] * 9,
        out_specs=pl.BlockSpec(memory_space=vmem),
        scratch_shapes=[
            vmem((block // LANES, block, LANES), BF16),
            vmem((block // LANES, block, LANES), BF16),
            vmem((2, depth, block), BF16),
            vmem((trials, block), F32),
            vmem((trials, block), F32),
            vmem((1, block), F32),
            vmem((1, projecting), jnp.int32),
            vmem((trials, block), F32),
            vmem((STEPS, chunks, trials, width), BF16),
            vmem((STEPS, chunks, trials, width), BF16),
            vmem((chunks, width, depth), BF16),
            pltpu.SMEM(delays.shape, jnp.int32),
            vmem(past_rates.shape[1:], BF16),
            vmem((STEPS - 1, packed, LANES), BF16),
            vmem((SUB, packed, LANES), BF16),
            vmem((STEPS + 2, packed, LANES), BF16),
            vmem((STEPS + 2, packed, LANES), BF16),
            dma((7,)),
            dma((2 * chunks,)),
            dma,
            dma((STEPS,)),
            dma((2,)),
            dma((STEPS,)),
        ],
        compiler_params=pltpu.CompilerParams(
            collective_id=0, has_side_effects=True, vmem_limit_bytes=66_000_000
        ),
        name="loop_dynamics",
    )(*(
        pltpu.with_memory_space_constraint(array, pltpu.HBM)
        for array in (delays, proj_index, past_rates, potential, stimulus, leak_rate, recurrence, ff_weight, fb_weight)
    ))


def solution(mesh):
    return jax.shard_map(
        functools.partial(local, mesh.shape["area"]),
        mesh=mesh,
        in_specs=(
            P("area", "row"),
            P("area", None),
            P("area", None, "groups", "row"),
            P("area", "groups", "row"),
            P("area", "groups", "row"),
            P("area", "row"),
            P("area", None, "row"),
            P("area", None, "row"),
            P("area", None, "row"),
        ),
        out_specs=P("area", "groups", "row"),
        check_vma=False,
    )
```
